32 devices in a mesh: img: 4 (over z), seq: 8 (over y, x, core).
Axes of the slice: x: 2, y: 2, z: 4, core: 2. Of those that a mesh axis runs over, the one named last changes fastest.
Arguments:
- tokens: bfloat16 [12288, 1024], P(('img', 'seq')), may hold values from -6 to 6
- segment_ids: int32 [12288], P('img'), may hold values from 0 to 2, as said below
- cotangent: bfloat16 [12288, 1024], P(('img', 'seq')), may hold values from -6 to 6
- attend_weight: float32 [1024, 3072], P(('img', 'seq'))
- output_weight: float32 [1024, 1024], P(('img', 'seq')), may hold values from -1.5 to 1.5
- expand_weight: float32 [1024, 4096], P(('img', 'seq')), may hold values from -0.1875 to 0.1875
- reduce_weight: float32 [4096, 1024], P(('img', 'seq')), may hold values from -0.09375 to 0.09375
- expand_bias: float32 [4096], P(('img', 'seq')), may hold values from -1 to 1
- vectors: float32 [10, 1024], P(None, ('img', 'seq'))
- attend_first: float32 [1024, 3072], P(('img', 'seq')), may hold values from -14 to 14
- attend_second: float32 [1024, 3072], P(('img', 'seq')), may hold values from 0.012288 to 4.9152
- output_first: float32 [1024, 1024], P(('img', 'seq')), may hold values from -14 to 14
- output_second: float32 [1024, 1024], P(('img', 'seq')), may hold values from 0.012288 to 4.9152
- expand_first: float32 [1024, 4096], P(('img', 'seq')), may hold values from -14 to 14
- expand_second: float32 [1024, 4096], P(('img', 'seq')), may hold values from 0.012288 to 4.9152
- reduce_first: float32 [4096, 1024], P(('img', 'seq')), may hold values from -14 to 14
- reduce_second: float32 [4096, 1024], P(('img', 'seq')), may hold values from 0.012288 to 4.9152
- bias_first: float32 [4096], P(('img', 'seq')), may hold values from -14 to 14
- bias_second: float32 [4096], P(('img', 'seq')), may hold values from 0.012288 to 4.9152
- vector_first: float32 [10, 1024], P(None, ('img', 'seq')), may hold values from -14 to 14
- vector_second: float32 [10, 1024], P(None, ('img', 'seq')), may hold values from 0.012288 to 4.9152
Outputs:
- block_output: bfloat16 [12288, 1024], P(('img', 'seq'))
- tokens_grad: bfloat16 [12288, 1024], P(('img', 'seq'))
- attend_grad: float32 [1024, 3072], P(('img', 'seq'))
- output_grad: float32 [1024, 1024], P(('img', 'seq'))
- expand_grad: float32 [1024, 4096], P(('img', 'seq'))
- reduce_grad: float32 [4096, 1024], P(('img', 'seq'))
- bias_grad: float32 [4096], P(('img', 'seq'))
- vector_grad: float32 [10, 1024], P(None, ('img', 'seq'))
- attend_updated: float32 [1024, 3072], P(('img', 'seq'))
- output_updated: float32 [1024, 1024], P(('img', 'seq'))
- expand_updated: float32 [1024, 4096], P(('img', 'seq'))
- reduce_updated: float32 [4096, 1024], P(('img', 'seq'))
- bias_updated: float32 [4096], P(('img', 'seq'))
- vector_updated: float32 [10, 1024], P(None, ('img', 'seq'))
- attend_first_new: float32 [1024, 3072], P(('img', 'seq'))
- attend_second_new: float32 [1024, 3072], P(('img', 'seq'))
- output_first_new: float32 [1024, 1024], P(('img', 'seq'))
- output_second_new: float32 [1024, 1024], P(('img', 'seq'))
- expand_first_new: float32 [1024, 4096], P(('img', 'seq'))
- expand_second_new: float32 [1024, 4096], P(('img', 'seq'))
- reduce_first_new: float32 [4096, 1024], P(('img', 'seq'))
- reduce_second_new: float32 [4096, 1024], P(('img', 'seq'))
- bias_first_new: float32 [4096], P(('img', 'seq'))
- bias_second_new: float32 [4096], P(('img', 'seq'))
- vector_first_new: float32 [10, 1024], P(None, ('img', 'seq'))
- vector_second_new: float32 [10, 1024], P(None, ('img', 'seq'))
The draws below stay inside these ranges and needn't reach their ends.
Inputs may be any that keep to these rules, and one draw needn't show every extreme that they name: `segment_ids`: within each group of 3072 rows, images of exactly 1370 rows are numbered 0, 1, and so on up to at most 1, and their rows stand at places of the group drawn at random; the remaining rows are padding with id 2. Every group holds one image or more, and some group holds 2.
All inputs are finite; a program needn't handle non-finite values.
Results may differ from the reference program's by a relative error of at most 0.033.
The reference program's roundings to bfloat16 on the way count: a program that leaves them out, or rounds other values in their place, can miss the bound.
Values may be sent and summed in bfloat16 or wider, within the bound.
No kernel may reach another device: no remote copies, remote signals or barrier semaphores. Data moves between devices by JAX's collectives and lax.ppermute only.
A program may use at most 256 MiB of HBM per device.

```python
import math
import jax
import jax.numpy as jnp
from jax import lax

D = 1024
H = 16
HD = 64
FF = 4096
IMG_LEN = 1370
VECS = 10
STEP = 3
GROUP = 3072
TOKENS = 12288
MAXIMG = 2
N_IMG = 4


def draw_segment_ids(key, part):
    groups = TOKENS // GROUP
    counts = jax.random.randint(key, (groups,), 1, MAXIMG + 1)
    forced = jax.random.randint(jax.random.fold_in(key, 7), (), 0, groups)
    counts = jnp.where(jnp.arange(groups, dtype=jnp.int32) == forced, MAXIMG, counts)
    place = jnp.arange(GROUP, dtype=jnp.int32) // IMG_LEN
    ids = jnp.where(place[None, :] < counts[:, None], place[None, :], MAXIMG)
    group_keys = jax.random.split(jax.random.fold_in(key, 11), groups)
    orders = jax.vmap(lambda k: jax.random.permutation(k, GROUP))(group_keys)
    ids = jnp.take_along_axis(ids, orders.astype(jnp.int32), axis=1)
    return ids.reshape(TOKENS).astype(jnp.int32)


def draw_attend_weight(key, part):
    base = jax.random.normal(jax.random.fold_in(key, 1), (D, 3 * D), jnp.float32) * D ** (-0.5)
    return base


def draw_vectors(key, part):
    uniform_part = jax.random.uniform(jax.random.fold_in(key, 1), (VECS, D), jnp.float32)
    normal_part = jax.random.normal(jax.random.fold_in(key, 2), (VECS, D), jnp.float32)
    row_index = jnp.arange(VECS, dtype=jnp.int32)[:, None]
    gains = 0.6 + 0.8 * uniform_part
    scales = 0.3 + 0.7 * uniform_part
    shifts = 0.2 * jnp.clip(normal_part, -4.0, 4.0)
    is_gain = (row_index == 0) | (row_index == 6)
    is_scale = (row_index == 5) | (row_index == 9)
    return jnp.where(is_gain, gains, jnp.where(is_scale, scales, shifts))


def block_levels(own_key, dims, shards, low, top_value):
    loudness = 1.0
    for axis_at, shards_of in shards:
        heights = jax.random.uniform(jax.random.fold_in(jax.random.fold_in(own_key, 6), axis_at), (shards_of,), jnp.float32, low / len(shards), top_value / len(shards))
        loudness = loudness * jnp.repeat(jnp.exp(heights), dims[axis_at] // shards_of).reshape((-1,) + (1,) * (len(dims) - 1 - axis_at))
    return loudness


def bell_draw(key, shape, width, bound, pieces=(), kind=jnp.bfloat16):
    array = jax.random.normal(key, shape, jnp.float32) * width
    if len(pieces) > 0:
        array = block_levels(key, shape, pieces, -0.22, 0.18) * array
    return jnp.clip(array, min=-bound, max=bound).astype(kind)


def setup_inputs(seed: int = 0) -> dict:
    streams_of = jax.random.split(jax.random.key(seed), 22)
    return {
        "tokens": bell_draw(streams_of[0], (TOKENS, D), 1.0, 6.0, ((0, 32),)),
        "segment_ids": draw_segment_ids(jax.random.fold_in(streams_of[21], 71), 0),
        "cotangent": bell_draw(streams_of[2], (TOKENS, D), 1.0, 6.0, ((0, 32),)),
        "attend_weight": draw_attend_weight(jax.random.fold_in(streams_of[21], 71), 0),
        "output_weight": bell_draw(streams_of[4], (D, D), (D // 64) ** -0.5, 1.5, ((0, 32),), jnp.float32),
        "expand_weight": bell_draw(streams_of[5], (D, FF), D ** -0.5, 0.1875, ((0, 32),), jnp.float32),
        "reduce_weight": bell_draw(streams_of[6], (FF, D), FF ** -0.5, 0.09375, ((0, 32),), jnp.float32),
        "expand_bias": bell_draw(streams_of[7], (FF,), 0.2, 1.0, ((0, 32),), jnp.float32),
        "vectors": draw_vectors(jax.random.fold_in(streams_of[21], 71), 0),
        "attend_first": bell_draw(streams_of[9], (D, 3 * D), (0.02 * TOKENS ** 0.5), 14.0, ((0, 32),), jnp.float32),
        "attend_second": jnp.clip(jnp.exp(math.log(4.9152) - 5.9914646 * jax.random.uniform(streams_of[10], (D, 3 * D), jnp.float32) ** block_levels(streams_of[10], (D, 3 * D), ((0, 32),), -0.2, 0.2)), 0.012288, 4.9152),
        "output_first": bell_draw(streams_of[11], (D, D), (0.02 * TOKENS ** 0.5), 14.0, ((0, 32),), jnp.float32),
        "output_second": jnp.clip(jnp.exp(math.log(4.9152) - 5.9914646 * jax.random.uniform(streams_of[12], (D, D), jnp.float32) ** block_levels(streams_of[12], (D, D), ((0, 32),), -0.2, 0.2)), 0.012288, 4.9152),
        "expand_first": bell_draw(streams_of[13], (D, FF), (0.02 * TOKENS ** 0.5), 14.0, ((0, 32),), jnp.float32),
        "expand_second": jnp.clip(jnp.exp(math.log(4.9152) - 5.9914646 * jax.random.uniform(streams_of[14], (D, FF), jnp.float32) ** block_levels(streams_of[14], (D, FF), ((0, 32),), -0.2, 0.2)), 0.012288, 4.9152),
        "reduce_first": bell_draw(streams_of[15], (FF, D), (0.02 * TOKENS ** 0.5), 14.0, ((0, 32),), jnp.float32),
        "reduce_second": jnp.clip(jnp.exp(math.log(4.9152) - 5.9914646 * jax.random.uniform(streams_of[16], (FF, D), jnp.float32) ** block_levels(streams_of[16], (FF, D), ((0, 32),), -0.2, 0.2)), 0.012288, 4.9152),
        "bias_first": bell_draw(streams_of[17], (FF,), (0.02 * TOKENS ** 0.5), 14.0, ((0, 32),), jnp.float32),
        "bias_second": jnp.clip(jnp.exp(math.log(4.9152) - 5.9914646 * jax.random.uniform(streams_of[18], (FF,), jnp.float32) ** block_levels(streams_of[18], (FF,), ((0, 32),), -0.2, 0.2)), 0.012288, 4.9152),
        "vector_first": bell_draw(streams_of[19], (VECS, D), (0.02 * TOKENS ** 0.5), 14.0, ((1, 32),), jnp.float32),
        "vector_second": jnp.clip(jnp.exp(math.log(4.9152) - 5.9914646 * jax.random.uniform(streams_of[20], (VECS, D), jnp.float32) ** block_levels(streams_of[20], (VECS, D), ((1, 32),), -0.2, 0.2)), 0.012288, 4.9152),
    }


EPS = 1e-06
BETA_ONE = 0.9
BETA_TWO = 0.999
ADAM_EPS = 1e-08
RATE_MATRIX = 0.05
RATE_VECTOR = 0.25
DECAY = 0.04
NEGATIVE = -1e+30

@jax.custom_vjp
def low(v):
    return lax.optimization_barrier(v.astype(jnp.bfloat16)).astype(jnp.float32)

@jax.custom_vjp
def low_back(v):
    return v

def low_keep(v):
    return (low(v), None)

def low_pass(kept, grad):
    return (grad,)

def back_keep(v):
    return (v, None)

def back_low(kept, grad):
    return (low(grad),)
low.defvjp(low_keep, low_pass)
low_back.defvjp(back_keep, back_low)

def exact_dot(left_side, right_side):
    return jnp.dot(left_side, right_side, precision=lax.Precision.HIGHEST, preferred_element_type=jnp.float32)

def normed(values, norm_gain, norm_shift):
    center = values - lax.optimization_barrier(jnp.mean(values, axis=-1, keepdims=True))
    spread = lax.optimization_barrier(jnp.mean(center * center, axis=-1, keepdims=True))
    return center * lax.rsqrt(spread + EPS) * norm_gain + norm_shift

def attend(query_block, key_heads, value_heads, query_ids, key_ids):
    scores = jnp.einsum('qhd,khd->hqk', query_block, key_heads, precision=lax.Precision.HIGHEST) * HD ** (-0.5)
    scores = low_back(scores)
    allowed = (query_ids[:, None] == key_ids[None, :])[None]
    scores = jnp.where(allowed, scores, NEGATIVE)
    weights = low(jax.nn.softmax(scores, axis=-1))
    return jnp.einsum('hqk,khd->qhd', weights, value_heads, precision=lax.Precision.HIGHEST)

def forward(params, inputs, group_ids):
    attend_low, output_low, expand_low, reduce_low, bias_low, vector_low = [low(p) for p in params]
    h_one = low(normed(inputs, vector_low[0], vector_low[1]))
    projected = exact_dot(h_one, attend_low)
    queries = low(low_back(projected[:, :D] + vector_low[2]))
    key_rows = low(low_back(projected[:, D:2 * D]))
    value_rows = low(low_back(projected[:, 2 * D:] + vector_low[3]))
    query_len = min(512, GROUP)
    query_blocks = queries.reshape(GROUP // query_len, query_len, H, HD)
    id_blocks = group_ids.reshape(GROUP // query_len, query_len)
    key_heads = key_rows.reshape(GROUP, H, HD)
    value_heads = value_rows.reshape(GROUP, H, HD)

    def one_block(sliced):
        return attend(sliced[0], key_heads, value_heads, sliced[1], group_ids)
    heads = lax.map(jax.checkpoint(one_block), (query_blocks, id_blocks))
    heads = low(low_back(heads.reshape(GROUP, D)))
    branch = low_back(exact_dot(heads, output_low) + vector_low[4])
    middle = inputs + vector_low[5] * branch
    h_two = low(normed(middle, vector_low[6], vector_low[7]))
    inner = low_back(exact_dot(h_two, expand_low) + bias_low)
    hidden = low(jax.nn.gelu(inner, approximate=False))
    last = low_back(exact_dot(hidden, reduce_low) + vector_low[8])
    return middle + vector_low[9] * last

def adamw(weight, gradient, first_moment, second_moment, rate, decay):
    first_moment = BETA_ONE * first_moment + (1.0 - BETA_ONE) * gradient
    second_moment = BETA_TWO * second_moment + (1.0 - BETA_TWO) * gradient * gradient
    first_hat = first_moment / (1.0 - BETA_ONE ** STEP)
    second_hat = second_moment / (1.0 - BETA_TWO ** STEP)
    weight = weight - rate * (first_hat / (jnp.sqrt(second_hat) + ADAM_EPS) + decay * weight)
    return (weight, first_moment, second_moment)

def reference(tokens, segment_ids, cotangent, attend_weight, output_weight, expand_weight, reduce_weight, expand_bias, vectors, attend_first, attend_second, output_first, output_second, expand_first, expand_second, reduce_first, reduce_second, bias_first, bias_second, vector_first, vector_second):
    params = (attend_weight, output_weight, expand_weight, reduce_weight, expand_bias, vectors)
    moments = ((attend_first, attend_second), (output_first, output_second), (expand_first, expand_second), (reduce_first, reduce_second), (bias_first, bias_second), (vector_first, vector_second))
    group_inputs = tokens.astype(jnp.float32).reshape(N_IMG, GROUP, D)
    group_cots = cotangent.astype(jnp.float32).reshape(N_IMG, GROUP, D)
    group_ids = segment_ids.reshape(N_IMG, GROUP)
    zeros = tuple((jnp.zeros_like(p) for p in params))

    def group_step(totals, sliced):
        inputs, cots, ids = sliced

        def apply(param_list, values):
            return forward(param_list, values, ids)
        result, pull = jax.vjp(apply, params, inputs)
        live = (ids < MAXIMG).astype(jnp.float32)[:, None]
        param_grads, input_grad = pull(cots * live)
        totals = tuple((a + b for a, b in zip(totals, param_grads)))
        return (totals, (result.astype(jnp.bfloat16), input_grad.astype(jnp.bfloat16)))
    grads, (outputs, input_grads) = lax.scan(group_step, zeros, (group_inputs, group_cots, group_ids))
    rates = (RATE_MATRIX, RATE_MATRIX, RATE_MATRIX, RATE_MATRIX, RATE_VECTOR, RATE_VECTOR)
    decays = (DECAY, DECAY, DECAY, DECAY, 0.0, 0.0)
    updated = []
    states = []
    for index in range(6):
        weight, first_new, second_new = adamw(params[index], grads[index], moments[index][0], moments[index][1], rates[index], decays[index])
        updated.append(weight)
        states.append(first_new)
        states.append(second_new)
    return (outputs.reshape(TOKENS, D), input_grads.reshape(TOKENS, D), grads[0], grads[1], grads[2], grads[3], grads[4], grads[5], updated[0], updated[1], updated[2], updated[3], updated[4], updated[5], states[0], states[1], states[2], states[3], states[4], states[5], states[6], states[7], states[8], states[9], states[10], states[11])
```

```python
import functools

import jax
import jax.numpy as jnp
from jax import lax
from jax.experimental import pallas as pl
from jax.experimental.pallas import tpu as pltpu
from jax.sharding import PartitionSpec as P


H = 16
IMG_LEN = 1370
STEP = 3

EPS = 1e-06
BETA_ONE = 0.9
BETA_TWO = 0.999
ADAM_EPS = 1e-08
RATE_MATRIX = 0.05
RATE_VECTOR = 0.25
DECAY = 0.04
FAR = 1e30
BF = jnp.bfloat16
F32 = jnp.float32
FEATURES = 128


def dot_nn(left_side, right_side):
    return lax.dot_general(left_side, right_side, (((1,), (0,)), ((), ())), preferred_element_type=F32)


def dot_nt(left_side, right_side):
    return lax.dot_general(left_side, right_side, (((1,), (1,)), ((), ())), preferred_element_type=F32)


def dot_tn(left_side, right_side):
    return lax.dot_general(left_side, right_side, (((0,), (0,)), ((), ())), preferred_element_type=F32)


def standard(values):
    center = values - jnp.mean(values, axis=-1, keepdims=True)
    spread = jnp.mean(center * center, axis=-1, keepdims=True)
    inverse = lax.rsqrt(spread + EPS)
    return center * inverse, inverse


def norm_back(grad, gain, unit, inverse):
    t = grad * gain
    return inverse * (
        t - jnp.mean(t, axis=-1, keepdims=True) - unit * jnp.mean(t * unit, axis=-1, keepdims=True)
    )


def adamw(weight, gradient, first_moment, second_moment, rate, decay):
    first_moment = BETA_ONE * first_moment + (1.0 - BETA_ONE) * gradient
    second_moment = BETA_TWO * second_moment + (1.0 - BETA_TWO) * gradient * gradient
    first_hat = first_moment / (1.0 - BETA_ONE**STEP)
    second_hat = second_moment / (1.0 - BETA_TWO**STEP)
    weight = weight - rate * (first_hat / (jnp.sqrt(second_hat) + ADAM_EPS) + decay * weight)
    return (weight, first_moment, second_moment)


class Ring:
    def __init__(self, axis, size):
        self.axis = axis
        self.size = size
        self.bits = [1 << b for b in range(size.bit_length() - 1)]

    def swap(self, value, distance):
        return lax.ppermute(value, self.axis, [(i, i ^ distance) for i in range(self.size)])

    def place(self):
        return lax.axis_index(self.axis)

    def bit(self, distance):
        return (self.place() // distance) % 2

    def all_sum(self, value):
        for distance in self.bits:
            value = value + self.swap(value, distance)
        return value

    def gather_relative(self, chunk):
        held = {0: chunk}
        if self.size == 8:
            half = chunk.shape[0] // 2
            held[2] = self.swap(chunk, 2)
            held[4] = self.swap(chunk, 4)
            held[1] = self.swap(chunk, 1)
            top = self.swap(held[2][:half], 4)
            low = self.swap(held[4][half:], 2)
            held[3] = self.swap(held[2], 1)
            held[5] = self.swap(held[4], 1)
            held[6] = jnp.concatenate([top, low], axis=0)
            held[7] = self.swap(held[6], 1)
        else:
            for distance in reversed(self.bits):
                for r in list(held):
                    held[r ^ distance] = self.swap(held[r], distance)
        return [held[r] for r in range(self.size)]

    def scatter_relative(self, parts):
        parts = dict(enumerate(parts))
        if self.size == 8:
            half = parts[0].shape[0] // 2
            q = {r: parts[r] + self.swap(parts[r ^ 1], 1) for r in (6, 2, 4, 0)}
            top = self.swap(q[6][:half], 4)
            low = self.swap(q[6][half:], 2)
            two = jnp.concatenate([q[2][:half] + top, q[2][half:]], axis=0)
            four = jnp.concatenate([q[4][:half], q[4][half:] + low], axis=0)
            return q[0] + self.swap(two, 2) + self.swap(four, 4)
        for distance in self.bits:
            parts = {
                r: parts[r] + self.swap(parts[r ^ distance], distance)
                for r in parts
                if not r & distance
            }
        return parts[0]

    def exchange_relative(self, parts):
        return [parts[0]] + [self.swap(parts[r], r) for r in range(1, self.size)]

    def gather(self, chunk):
        value = chunk[None]
        for distance in reversed(self.bits):
            other = self.swap(value, distance)
            upper = self.bit(distance) == 1
            value = jnp.where(
                upper, jnp.stack([other, value], 1), jnp.stack([value, other], 1)
            )
            value = value.reshape((-1,) + chunk.shape)
        return value

    def scatter(self, value):
        for distance in self.bits:
            shape = value.shape
            value = value.reshape((shape[0] // 2, 2) + shape[1:])
            bit = self.bit(distance)
            kept = lax.dynamic_index_in_dim(value, bit, 1, keepdims=False)
            sent = lax.dynamic_index_in_dim(value, 1 - bit, 1, keepdims=False)
            value = kept + self.swap(sent, distance)
        return value[0]


def attention_forward_kernel(heads, q_ref, fq_ref, k_ref, fk_ref, v_ref, o_ref, low_ref, lse_ref, wide):
    width = q_ref.shape[1]

    @pl.when(pl.program_id(0) == 0)
    def _():
        wide[:, :width] = k_ref[...]
        wide[:, width:] = fk_ref[...]

    size = width // heads
    query = q_ref[...] * (size**-0.5)
    lane = lax.broadcasted_iota(jnp.int32, query.shape, 1) // size
    lse_lane = lax.broadcasted_iota(jnp.int32, lse_ref.shape, 1)
    out = jnp.zeros(o_ref.shape, F32)
    lse_out = jnp.zeros(lse_ref.shape, F32)
    for h in range(heads):
        own = jnp.where(lane == h, query, jnp.zeros_like(query)).astype(BF)
        scores = dot_nt(jnp.concatenate([own, fq_ref[...]], axis=1), wide[...])
        top = jnp.max(scores, axis=1, keepdims=True)
        weights = jnp.exp(scores - top)
        total = jnp.sum(weights, axis=1, keepdims=True)
        result = dot_nn(weights.astype(BF), v_ref[...]) / total
        out = jnp.where(lane == h, result, out)
        lse_out = jnp.where(lse_lane == h, top + jnp.log(total), lse_out)
    o_ref[...] = out
    low_ref[...] = out.astype(BF)
    lse_ref[...] = lse_out


def attention_forward(q, k, v, fq, fk, heads, block):
    rows, width = q.shape
    part = lambda columns: pl.BlockSpec((block, columns), lambda i: (i, 0))
    full = lambda columns: pl.BlockSpec((rows, columns), lambda i: (0, 0))
    return pl.pallas_call(
        functools.partial(attention_forward_kernel, heads),
        grid=(rows // block,),
        in_specs=[part(width), part(FEATURES), full(width), full(FEATURES), full(width)],
        out_specs=[part(width), part(width), part(128)],
        out_shape=[
            jax.ShapeDtypeStruct((rows, width), F32),
            jax.ShapeDtypeStruct((rows, width), BF),
            jax.ShapeDtypeStruct((rows, 128), F32),
        ],
        scratch_shapes=[pltpu.VMEM((rows, width + FEATURES), BF)],
        compiler_params=pltpu.CompilerParams(
            dimension_semantics=("arbitrary",), vmem_limit_bytes=56 * 1024 * 1024
        ),
        name="attention_forward",
    )(q, fq, k, fk, v)


def attention_backward_kernel(
    heads, q_ref, fq_ref, g_ref, o_ref, lse_ref, k_ref, fk_ref, v_ref, da_ref, wide, dk, dv
):
    step = pl.program_id(0)
    width = q_ref.shape[1]
    block = q_ref.shape[0]

    @pl.when(step == 0)
    def _():
        wide[:, :width] = k_ref[...]
        wide[:, width:] = fk_ref[...]
        dk[...] = jnp.zeros_like(dk)
        dv[...] = jnp.zeros_like(dv)

    size = width // heads
    scale = size**-0.5
    query = q_ref[...] * scale
    grad = g_ref[...]
    lane = lax.broadcasted_iota(jnp.int32, query.shape, 1) // size
    lse_lane = lax.broadcasted_iota(jnp.int32, lse_ref.shape, 1)
    product = grad.astype(F32) * o_ref[...]
    query_turned = query.astype(F32).T.astype(BF)
    grad_turned = grad.astype(F32).T.astype(BF)
    dq = jnp.zeros(query.shape, F32)
    for h in range(heads):
        own = jnp.where(lane == h, query, jnp.zeros_like(query)).astype(BF)
        own_grad = jnp.where(lane == h, grad, jnp.zeros_like(grad))
        lse = jnp.sum(jnp.where(lse_lane == h, lse_ref[...], 0.0), axis=1, keepdims=True)
        delta = jnp.sum(jnp.where(lane == h, product, 0.0), axis=1, keepdims=True)
        scores = dot_nt(jnp.concatenate([own, fq_ref[...]], axis=1), wide[...])
        weights = jnp.exp(scores - lse)
        slope = weights * (dot_nt(own_grad, v_ref[...]) - delta)
        slope_low = slope.astype(BF)
        dq = jnp.where(lane == h, dot_nn(slope_low, k_ref[...]) * scale, dq)
        span = slice(h * size, (h + 1) * size)
        dk[span, :] += dot_nn(query_turned[span, :], slope_low)
        dv[span, :] += dot_nn(grad_turned[span, :], weights.astype(BF))
    rows = pl.ds(pl.multiple_of(step * block, block), block)
    da_ref[rows, :width] = dq.astype(BF)

    @pl.when(step == pl.num_programs(0) - 1)
    def _():
        da_ref[:, width : 2 * width] = dk[...].T.astype(BF)
        da_ref[:, 2 * width :] = dv[...].T.astype(BF)


def attention_backward(q, k, v, fq, fk, grad, out, lse, heads, block):
    rows, width = q.shape
    part = lambda columns: pl.BlockSpec((block, columns), lambda i: (i, 0))
    full = lambda columns: pl.BlockSpec((rows, columns), lambda i: (0, 0))
    return pl.pallas_call(
        functools.partial(attention_backward_kernel, heads),
        grid=(rows // block,),
        in_specs=[
            part(width),
            part(FEATURES),
            part(width),
            part(width),
            part(128),
            full(width),
            full(FEATURES),
            full(width),
        ],
        out_specs=full(3 * width),
        out_shape=jax.ShapeDtypeStruct((rows, 3 * width), BF),
        scratch_shapes=[
            pltpu.VMEM((rows, width + FEATURES), BF),
            pltpu.VMEM((width, rows), F32),
            pltpu.VMEM((width, rows), F32),
        ],
        compiler_params=pltpu.CompilerParams(
            dimension_semantics=("arbitrary",), vmem_limit_bytes=60 * 1024 * 1024
        ),
        name="attention_backward",
    )(q, fq, grad, out, lse, k, fk, v)


def shards(
    img_size,
    seq_size,
    tokens,
    segment_ids,
    cotangent,
    attend_weight,
    output_weight,
    expand_weight,
    reduce_weight,
    expand_bias,
    vectors,
    attend_first,
    attend_second,
    output_first,
    output_second,
    expand_first,
    expand_second,
    reduce_first,
    reduce_second,
    bias_first,
    bias_second,
    vector_first,
    vector_second,
):
    img = Ring("img", img_size)
    seq = Ring("seq", seq_size)
    rows, width = tokens.shape
    group = segment_ids.shape[0]
    image_most = group // IMG_LEN
    kinds = image_most + 1
    heads = H // seq_size
    own_width = width // seq_size
    own_slice = attend_weight.shape[0]
    hidden = expand_weight.shape[1]
    strip = hidden // (img_size * seq_size)
    own_hidden = img_size * strip
    seq_place = seq.place()
    img_place = img.place()
    device_place = img_place * seq_size + seq_place

    x_parts = seq.gather_relative(tokens)

    small = jnp.zeros((vectors.shape[0] + hidden // width, width), BF)
    small = lax.dynamic_update_slice(
        small, vectors.astype(BF), (0, device_place * vectors.shape[1])
    )
    bias_rows = lax.dynamic_update_slice(
        jnp.zeros((hidden,), BF), expand_bias.astype(BF), (device_place * strip,)
    ).reshape(-1, width)
    small = small + jnp.pad(bias_rows, ((vectors.shape[0], 0), (0, 0)))
    small = img.all_sum(seq.all_sum(small))
    vector_rows = small[: vectors.shape[0]].astype(F32)
    bias_own = (
        lax.dynamic_index_in_dim(
            small[vectors.shape[0] :].reshape(img_size, seq_size, strip), seq_place, 1, keepdims=False
        )
        .reshape(own_hidden)
        .astype(F32)
    )
    g_one, c_one, b_q, b_v, b_o, s_one, g_two, c_two, b_r, s_two = [
        vector_rows[i] for i in range(10)
    ]

    attend_cut = attend_weight.astype(BF).reshape(own_slice, 3, seq_size, own_width)
    attend_cut = attend_cut.transpose(2, 0, 1, 3).reshape(seq_size, own_slice, 3 * own_width)
    expand_cut = expand_weight.astype(BF).reshape(own_slice, img_size, seq_size, strip)
    expand_cut = expand_cut.transpose(2, 0, 1, 3).reshape(seq_size, own_slice, own_hidden)
    cut = jnp.concatenate([attend_cut, expand_cut], axis=2)
    cut = lax.all_to_all(cut, "seq", split_axis=0, concat_axis=0)
    cut = cut.reshape(seq_size * own_slice, 3 * own_width + own_hidden)
    attend_own = img.gather(cut[:, : 3 * own_width]).reshape(width, 3 * own_width)
    expand_own = img.gather(cut[:, 3 * own_width :]).reshape(width, own_hidden)
    reduce_own = img.gather(reduce_weight.astype(BF)).reshape(own_hidden, width)

    output_img = img.gather(output_weight.astype(BF))
    output_parts = seq.gather_relative(output_img.reshape(-1, width))
    order = jnp.arange(seq_size) ^ seq_place
    output_all = jnp.stack(output_parts).reshape(seq_size, img_size, own_slice, width)
    output_all = jnp.take(output_all, order, axis=0).transpose(1, 0, 2, 3)
    output_all = jnp.take(output_all.reshape(seq_size, own_width, width), order, axis=0)
    output_all = output_all.reshape(width, width)

    residual_in = tokens.astype(F32)
    own_ids = lax.dynamic_slice_in_dim(segment_ids, seq_place * rows, rows)
    group_ids = jnp.take(segment_ids.reshape(seq_size, rows), order, axis=0).reshape(group)
    feature = lax.broadcasted_iota(jnp.int32, (group, FEATURES), 1)
    same = feature == group_ids[:, None]
    query_feature = jnp.where(same, FAR, 0.0).astype(BF)
    key_feature = jnp.where((feature < kinds) & ~same, -1.0, 0.0).astype(BF)

    live_rows = (own_ids < image_most).astype(F32)[:, None]
    grad_out = cotangent.astype(F32) * live_rows
    grad_last = (grad_out * s_two).astype(BF)
    grad_last_parts = seq.gather_relative(grad_last)

    x_all = jnp.concatenate(x_parts, axis=0).astype(F32)
    unit_all, _ = standard(x_all)
    h_one = (unit_all * g_one + c_one).astype(BF)
    projected = dot_nn(h_one, attend_own)
    b_q_own = lax.dynamic_slice_in_dim(b_q, seq_place * own_width, own_width)
    b_v_own = lax.dynamic_slice_in_dim(b_v, seq_place * own_width, own_width)
    own_query = (projected[:, :own_width] + b_q_own).astype(BF)
    own_key = projected[:, own_width : 2 * own_width].astype(BF)
    own_value = (projected[:, 2 * own_width :] + b_v_own).astype(BF)
    out_exact, out_low, lse = attention_forward(
        own_query, own_key, own_value, query_feature, key_feature, heads, 256
    )
    out_cut = out_low.reshape(seq_size, rows, own_width)
    heads_parts = seq.exchange_relative([out_cut[r] for r in range(seq_size)])
    heads_low = jnp.concatenate(heads_parts, axis=1)
    branch = dot_nn(heads_low, output_all) + b_o
    middle = residual_in + s_one * branch
    unit_two, inverse_two = standard(middle)
    h_two = (unit_two * g_two + c_two).astype(BF)

    h_two_all = jnp.concatenate(seq.gather_relative(h_two), axis=0)
    grad_last_all = jnp.concatenate(grad_last_parts, axis=0)
    inner = dot_nn(h_two_all, expand_own) + bias_own
    erf_part = lax.erf(inner * (0.5**0.5))
    cumulative = 0.5 * (1.0 + erf_part)
    hidden_low = (inner * cumulative).astype(BF)
    density = jnp.exp(-0.5 * inner * inner) * (0.3989422804014327)
    grad_inner = dot_nt(grad_last_all, reduce_own) * (cumulative + inner * density)
    grad_inner_low = grad_inner.astype(BF)
    grad_two_terms = dot_nt(grad_inner_low, expand_own).astype(BF).reshape(seq_size, rows, width)
    grad_h_two = seq.scatter_relative([grad_two_terms[r] for r in range(seq_size)]).astype(F32)

    last_terms = dot_nn(hidden_low, reduce_own).astype(BF).reshape(seq_size, rows, width)
    last = seq.scatter_relative([last_terms[r] for r in range(seq_size)]).astype(F32) + b_r
    block_output = (middle + s_two * last).astype(BF)
    grad_scale_two = jnp.sum(grad_out * last, axis=0)
    grad_reduce_bias = jnp.sum(grad_last.astype(F32), axis=0)

    grad_reduce_own = dot_tn(hidden_low, grad_last_all)
    grad_expand_own = dot_tn(h_two_all, grad_inner_low)
    grad_bias_own = jnp.sum(grad_inner_low.astype(F32), axis=0)

    grad_gain_two = jnp.sum(grad_h_two * unit_two, axis=0)
    grad_shift_two = jnp.sum(grad_h_two, axis=0)
    grad_middle = grad_out + norm_back(grad_h_two, g_two, unit_two, inverse_two)
    grad_scale_one = jnp.sum(grad_middle * branch, axis=0)
    grad_branch = (grad_middle * s_one).astype(BF)
    grad_output_bias = jnp.sum(grad_branch.astype(F32), axis=0)
    grad_heads = dot_nt(grad_branch, output_all).astype(BF)
    grad_cut = [grad_heads[:, r * own_width : (r + 1) * own_width] for r in range(seq_size)]
    grad_own = jnp.concatenate(seq.exchange_relative(grad_cut), axis=0)
    grad_output_terms = dot_tn(heads_low, grad_branch)

    grad_projected = attention_backward(
        own_query,
        own_key,
        own_value,
        query_feature,
        key_feature,
        grad_own,
        out_exact,
        lse,
        heads,
        256,
    )
    grad_one_terms = dot_nt(grad_projected, attend_own)
    grad_gain_one = jnp.sum(grad_one_terms * unit_all, axis=0)
    grad_shift_one = jnp.sum(grad_one_terms, axis=0)
    grad_one_low = grad_one_terms.astype(BF).reshape(seq_size, rows, width)
    grad_h_one = seq.scatter_relative([grad_one_low[r] for r in range(seq_size)]).astype(F32)
    unit_one, inverse_one = standard(residual_in)
    tokens_grad = (grad_middle + norm_back(grad_h_one, g_one, unit_one, inverse_one)).astype(BF)
    grad_attend_own = dot_tn(h_one, grad_projected)

    attend_sum = img.scatter(grad_attend_own.astype(BF).reshape(img_size, -1, 3 * own_width))
    expand_sum = img.scatter(grad_expand_own.astype(BF).reshape(img_size, -1, own_hidden))
    both = jnp.concatenate([attend_sum, expand_sum], axis=1)
    both = both.reshape(seq_size, own_slice, 3 * own_width + own_hidden)
    both = lax.all_to_all(both, "seq", split_axis=0, concat_axis=0).astype(F32)
    attend_grad = both[:, :, : 3 * own_width].reshape(seq_size, own_slice, 3, own_width)
    attend_grad = attend_grad.transpose(1, 2, 0, 3).reshape(own_slice, 3 * width)
    expand_grad = both[:, :, 3 * own_width :].reshape(seq_size, own_slice, img_size, strip)
    expand_grad = expand_grad.transpose(1, 2, 0, 3).reshape(own_slice, hidden)
    reduce_grad = img.scatter(grad_reduce_own.astype(BF).reshape(img_size, strip, width))
    reduce_grad = reduce_grad.astype(F32)
    output_terms = jnp.take(
        grad_output_terms.astype(BF).reshape(seq_size, own_width, width), order, axis=0
    )
    output_terms = output_terms.reshape(img_size, seq_size, own_slice, width).transpose(1, 0, 2, 3)
    output_terms = jnp.take(output_terms, order, axis=0)
    output_sum = seq.scatter_relative([
        output_terms[r].reshape(img_size * own_slice, width) for r in range(seq_size)
    ])
    output_grad = img.scatter(output_sum.reshape(img_size, own_slice, width)).astype(F32)

    column_sums = jnp.sum(grad_projected.astype(F32), axis=0)
    spread_out = lambda part: lax.dynamic_update_slice(
        jnp.zeros((width,), F32), part, (seq_place * own_width,)
    )
    bias_spread = lax.dynamic_update_slice(
        jnp.zeros((img_size, seq_size, strip), F32),
        grad_bias_own.reshape(img_size, 1, strip),
        (0, seq_place, 0),
    ).reshape(-1, width)
    sums = jnp.concatenate(
        [
            jnp.stack(
                [
                    grad_gain_one,
                    grad_shift_one,
                    spread_out(column_sums[:own_width]),
                    spread_out(column_sums[2 * own_width :]),
                    grad_output_bias,
                    grad_scale_one,
                    grad_gain_two,
                    grad_shift_two,
                    grad_reduce_bias,
                    grad_scale_two,
                ]
            ),
            bias_spread,
        ],
        axis=0,
    )
    sums = img.all_sum(seq.all_sum(sums))
    vector_grad = lax.dynamic_slice_in_dim(
        sums[: vectors.shape[0]], device_place * vectors.shape[1], vectors.shape[1], axis=1
    )
    bias_grad = lax.dynamic_slice_in_dim(
        sums[vectors.shape[0] :].reshape(hidden), device_place * strip, strip
    )

    owned = (attend_grad, output_grad, expand_grad, reduce_grad, bias_grad, vector_grad)
    params = (attend_weight, output_weight, expand_weight, reduce_weight, expand_bias, vectors)
    moments = (
        (attend_first, attend_second),
        (output_first, output_second),
        (expand_first, expand_second),
        (reduce_first, reduce_second),
        (bias_first, bias_second),
        (vector_first, vector_second),
    )
    rates = (RATE_MATRIX, RATE_MATRIX, RATE_MATRIX, RATE_MATRIX, RATE_VECTOR, RATE_VECTOR)
    decays = (DECAY, DECAY, DECAY, DECAY, 0.0, 0.0)
    updated = []
    states = []
    for index in range(6):
        weight, first_new, second_new = adamw(
            params[index],
            owned[index],
            moments[index][0],
            moments[index][1],
            rates[index],
            decays[index],
        )
        updated.append(weight)
        states.append(first_new)
        states.append(second_new)
    return (block_output, tokens_grad, *owned, *updated, *states)


def solution(mesh):
    both = ("img", "seq")
    matrix = P(both, None)
    line = P(both)
    columns = P(None, both)
    placed = (
        (matrix, P("img"), matrix)
        + (matrix,) * 4
        + (line, columns)
        + (matrix,) * 8
        + (line, line, columns, columns)
    )
    weights = (matrix,) * 4 + (line, columns)
    out = (matrix, matrix) + weights + weights + (matrix,) * 8 + (line, line, columns, columns)
    return jax.shard_map(
        functools.partial(shards, mesh.shape["img"], mesh.shape["seq"]),
        mesh=mesh,
        in_specs=placed,
        out_specs=out,
        check_vma=False,
    )
```
